256 devices in a mesh: delay: 16 (over z, y_hi), row: 2 (over core), col: 8 (over y_lo, x).
Axes of the slice: x: 4, y: 4 (y_hi: 2, y_lo: 2; y = y_hi * 2 + y_lo), z: 8, core: 2. Of those that a mesh axis runs over, the one named last changes fastest.
Arguments:
- delays: float32 [16, 4096, 2, 2048], P('delay', 'row', None, 'col'), may hold values from -0.01171875 to 0.01171875
- history: float32 [16, 256, 4096], P('delay', None, ('row', 'col')), may hold values from -6 to 6
- sources: float32 [4, 256, 4096], P(None, None, ('row', 'col')), may hold values from -6 to 6
- self_inverse: float32 [16, 256, 256], P(('row', 'col')), may hold values from -4 to 4, as said below
Outputs:
- adjoints: float32 [4, 256, 4096], P(None, None, ('row', 'col'))
The draws below stay inside these ranges and needn't reach their ends.
Inputs may be any that keep to these rules, and one draw needn't show every extreme that they name: `self_inverse`: dense blocks.
All inputs are finite; a program needn't handle non-finite values.
Results may differ from the reference program's by a relative error of at most 0.0001.
Values sent between devices are 32-bit elements; how exact they have to be, the bound alone decides.
No kernel may reach another device: no remote copies, remote signals or barrier semaphores. Data moves between devices by JAX's collectives and lax.ppermute only.
A program may use at most 64 MiB of HBM per device.

```python
import jax
import jax.numpy as jnp
from jax import lax

N = 4096
R = 256
S = 256
STEPS = 4
K = 16
BLOCKS = 16
N_ROW = 2


def draw_self_inverse(key, part):
    noise = jax.random.normal(jax.random.fold_in(key, 11), (N // S, S, S), jnp.float32)
    blocks = jnp.eye(S, dtype=jnp.float32)[None] + 0.6 * noise / jnp.sqrt(jnp.float32(S))
    return jnp.clip(blocks, -4.0, 4.0)


def level_of(rng, dims, split, smallest, largest):
    def one(dim, shards_of):
        draws = jax.random.uniform(jax.random.fold_in(jax.random.fold_in(rng, 6), dim), (shards_of,), jnp.float32, smallest / len(split), largest / len(split))
        return jnp.repeat(jnp.exp(draws), dims[dim] // shards_of).reshape((-1,) + (1,) * (len(dims) - dim - 1))

    factor_of = one(*split[0])
    for cut in split[1:]:
        factor_of = factor_of * one(*cut)
    return factor_of


def scatter_about(rng, shape, spread, bound, shards=(), held_as=jnp.bfloat16):
    level = level_of(rng, shape, shards, -0.22, 0.18) if shards else 1.0
    values = jax.random.normal(rng, shape, jnp.float32) * spread * level
    return jnp.minimum(jnp.maximum(values, -bound), bound).astype(held_as)


def setup_inputs(seed: int = 0) -> dict:
    keys = jax.random.split(jax.random.key(seed), 5)
    return {
        "delays": scatter_about(keys[0], (K, N, N_ROW, N // N_ROW), (4 * N * K) ** -0.5, 0.01171875, ((0, 16), (1, 2), (3, 8)), jnp.float32),
        "history": scatter_about(keys[1], (K, R, N), 1.0, 6.0, ((0, 16), (2, 16)), jnp.float32),
        "sources": scatter_about(keys[2], (STEPS, R, N), 1.0, 6.0, ((2, 16),), jnp.float32),
        "self_inverse": draw_self_inverse(jax.random.fold_in(keys[4], 71), 0),
    }


def reference(delays, history, sources, self_inverse):
    mats = delays.reshape(K, N, N)
    highest = lax.Precision.HIGHEST

    def add_delay(total, pair):
        hist_k, mat_k = pair
        return total + jnp.einsum("rj,ij->ri", hist_k, mat_k, precision=highest), None

    def one_step(hist, source):
        coupled, unused = lax.scan(add_delay, jnp.zeros((R, N), jnp.float32), (hist, mats))
        drive = (source - coupled).reshape(R, BLOCKS, S)
        adjoint = jnp.einsum("rbs,bst->rbt", drive, self_inverse, precision=highest).reshape(R, N)
        hist = jnp.concatenate([adjoint[None], hist[:-1]], axis=0)
        return hist, adjoint

    final, adjoints = lax.scan(one_step, history, sources)
    return adjoints
```

```python
import jax
import jax.numpy as jnp
from jax import lax
from jax.experimental import pallas as pl
from jax.experimental.pallas import tpu as pltpu
from jax.sharding import PartitionSpec as P


AXES = ("delay", "row", "col")
NX, NY, NZ, CORES = 4, 4, 8, 2
F32 = jnp.float32
VMEM = pl.BlockSpec(memory_space=pltpu.VMEM)
SMEM = pl.BlockSpec(memory_space=pltpu.SMEM)


def flat(x, y, z, core):
    return ((z * 2 + y // 2) * CORES + core) * 8 + (y % 2) * 4 + x


CHIPS = [
    (x, y, z, core)
    for x in range(NX)
    for y in range(NY)
    for z in range(NZ)
    for core in range(CORES)
]


def move(values, to):
    pairs = []
    for x, y, z, core in CHIPS:
        target = to(x, y, z)
        if target is not None:
            pairs.append((flat(x, y, z, core), flat(*target, core)))
    return lax.ppermute(values, AXES, pairs)


def along_x(values, by):
    return move(values, lambda x, y, z: ((x + by) % NX, y, z))


def along_y(values, by):
    return move(values, lambda x, y, z: (x, (y + by) % NY, z))


def along_z(values, by):
    return move(values, lambda x, y, z: (x, y, (z + by) % NZ))


def swap_half(values):
    return move(values, lambda x, y, z: (x, (y + 2) % NY, z))


def swap_core(values):
    return lax.ppermute(values, "row", [(0, 1), (1, 0)])


Z_GROUPS = [[2 * z + half for z in range(NZ)] for half in range(2)]


def z_exchange(values):
    return lax.all_to_all(values, "delay", 0, 0, axis_index_groups=Z_GROUPS)


def col_exchange(values):
    return lax.all_to_all(values, "col", 0, 0)


def halves(a):
    high = a.astype(jnp.bfloat16)
    return high, (a - high.astype(F32)).astype(jnp.bfloat16)


def product(a, b, dims):
    a1, a2 = halves(a)
    b1, b2 = halves(b)

    def dot(p, q):
        return lax.dot_general(p, q, (dims, ((), ())), preferred_element_type=F32)

    return dot(a1, b1) + (dot(a1, b2) + dot(a2, b1))


def chunk_kernel(count, table, tile_ref, own_ref, other_ref, *outs):
    g = pl.program_id(0)
    core = table[0]
    first = jnp.concatenate([own_ref[0], own_ref[1]], axis=0)
    second = jnp.concatenate([other_ref[0], other_ref[1]], axis=0)
    mine = tile_ref[:, pl.ds(pl.multiple_of(core * 256, 256), 256)]
    theirs = tile_ref[:, pl.ds(pl.multiple_of((1 - core) * 256, 256), 256)]
    value = product(mine, first, ((1,), (1,))) + product(theirs, second, ((1,), (1,)))
    for k in range(count):

        @pl.when(g // 2 == k)
        def _(k=k):
            outs[k][0] = value


def chunks(core, blocks, rows, tile, own, other):
    count = len(blocks) // 2
    table = jnp.stack([jnp.int32(core), *[jnp.int32(v) for pair in zip(blocks, rows) for v in pair]])
    pieces = pl.BlockSpec((2, 128, 256), lambda g, t: (0, t[2 + 2 * g], 0))
    return pl.pallas_call(
        lambda *refs: chunk_kernel(count, *refs),
        out_shape=[jax.ShapeDtypeStruct((2, 256, 256), F32)] * count,
        grid_spec=pltpu.PrefetchScalarGridSpec(
            num_scalar_prefetch=1,
            grid=(2 * count,),
            in_specs=[pl.BlockSpec((256, 512), lambda g, t: (t[1 + 2 * g], 0)), pieces, pieces],
            out_specs=[
                pl.BlockSpec((1, 256, 256), lambda g, t, k=k: (jnp.clip(g - 2 * k, 0, 1), 0, 0))
                for k in range(count)
            ],
        ),
        cost_estimate=pl.CostEstimate(
            flops=2 * count * 3 * 2 * 256 * 512 * 256, transcendentals=0, bytes_accessed=2 * count * 1280 * 1024
        ),
    )(table, tile, own, other)


def call(body, shapes, *args):
    specs = [SMEM if a.ndim == 1 else VMEM for a in args]
    single = not isinstance(shapes, list)
    listed = [shapes] if single else shapes
    out = pl.pallas_call(
        body,
        out_shape=[jax.ShapeDtypeStruct(s, F32) for s in listed],
        in_specs=specs,
        out_specs=[VMEM] * len(listed),
    )(*args)
    return out[0] if single else out


def meet_kernel(place, mine_a, mine_b, up_a, up_b, down_a, down_b, far_a, far_b, near, last, base):
    me = place[0]
    for j in range(4):
        part = lax.rem(me + j, 4)
        block, second = lax.rem(part, 2), part // 2 == 1

        def put(total):
            if j == 0:
                base[...] = total
            elif j == 2:
                far_a[...] = total[:128]
                far_b[...] = total[128:]
            else:
                near_or_last = near if j == 1 else last
                near_or_last[...] = total

        @pl.when(second)
        def _():
            put(mine_b[block] + up_b[block] + down_b[block])

        @pl.when(jnp.logical_not(second))
        def _():
            put(mine_a[block] + up_a[block] + down_a[block])


def meet(me, *pieces):
    return call(
        meet_kernel, [(128, 256), (128, 256), (256, 256), (256, 256), (256, 256)], me[None], *pieces
    )


def second_ring(pieces, shift):
    far_a, far_b, near, last, base = pieces
    u = shift(far_a, 1)
    v = shift(far_b, -1)
    up = shift(jnp.concatenate([near[:128] + u, near[128:]], axis=0), 1)
    down = shift(jnp.concatenate([last[:128], last[128:] + v], axis=0), -1)
    return base + up + down


def turn_kernel(place, sources, out, scratch):
    half, z = place[0], place[1]
    for s in range(4):
        scratch[...] = sources[s, pl.ds(pl.multiple_of(half * 128, 128), 128), :].T
        out[s] = scratch[pl.ds(pl.multiple_of(z * 32, 32), 32), :]


def drives_kernel(spread, sources, first, rest):
    given = spread[0]
    for k in range(1, 8):
        given = given + spread[k]
    for s in range(4):
        drive = sources[s] - given[:, s * 128 : s * 128 + 128]
        if s == 0:
            for k in range(8):
                first[k] = drive
        else:
            rest[s - 1] = drive


def drive_kernel(came, rest, out, *, step):
    total = came[0]
    for k in range(1, 8):
        total = total + came[k]
    drive = rest[step - 1] - total
    for k in range(8):
        out[k] = drive


def inverse_kernel(drive, inverse, turned, plain):
    d = drive[...].reshape(256, 128)
    m = inverse[0]
    turned[...] = product(m, d, ((0,), (0,)))
    plain[...] = turned[...].T


def coupled_kernel(place, *refs):
    core = place[0]
    out = refs[-1]
    terms = (len(refs) - 1) // 3
    total = None
    for t in range(terms):
        w, own, other = refs[3 * t : 3 * t + 3]
        mine = w[:, pl.ds(pl.multiple_of(core * 256, 256), 256)]
        theirs = w[:, pl.ds(pl.multiple_of((1 - core) * 256, 256), 256)]
        value = product(mine, own[...], ((1,), (0,))) + product(theirs, other[...], ((1,), (0,)))
        total = value if total is None else total + value
    out[...] = total.reshape(8, 32, 128)


def on_device(delays, history, sources, self_inverse):
    d = lax.axis_index("delay")
    core = lax.axis_index("row")
    c = lax.axis_index("col")
    z, half = d // 2, lax.rem(d, 2)
    x, low = lax.rem(c, 4), c // 4
    y = half * 2 + low

    own = history[0]
    shifted = [own] + [
        lax.ppermute(own, "delay", [(i, i + k) for i in range(16 - k)]) for k in range(1, 4)
    ]
    tile = delays.reshape(2048, 512)
    place = jnp.stack([half, z])
    mine = pl.pallas_call(
        turn_kernel,
        out_shape=jax.ShapeDtypeStruct((4, 32, 128), F32),
        in_specs=[SMEM, VMEM],
        out_specs=VMEM,
        scratch_shapes=[pltpu.VMEM((256, 128), F32)],
    )(place, sources)

    own_x, own_y = jnp.stack(shifted[:2]), jnp.stack(shifted[2:])
    other_x, other_y = swap_core(own_x), swap_core(own_y)

    def x_chunk(j):
        to = lax.rem(x + j, 4)
        return [to, to + 4]

    def y_chunk(j):
        to = lax.rem(y + j, 4)
        blocks = [lax.rem(to, 2) * 4 + k for k in range(4)]
        return blocks, [to // 2] * 4

    far_a, far_b = chunks(core, x_chunk(2) * 2, [0, 0, 1, 1], tile, own_x, other_x)
    u, v = along_x(far_a, 1), along_x(far_b, -1)
    blocks, rows = y_chunk(2)
    far_c, far_d = chunks(core, blocks, rows, tile, own_y, other_y)
    w, q = along_y(far_c, 1), along_y(far_d, -1)

    n1b, n3a, n1a, n3b, ma, mb = chunks(
        core,
        x_chunk(1) + x_chunk(3) + x_chunk(1) + x_chunk(3) + x_chunk(0) * 2,
        [1, 1, 0, 0, 0, 0, 1, 1, 0, 0, 1, 1],
        tile,
        own_x,
        other_x,
    )
    up_b, down_a = along_x(n1b, 1), along_x(n3a, -1)
    (b1, r1), (b3, r3), (b0, r0) = y_chunk(1), y_chunk(3), y_chunk(0)
    n1d, n3c, n1c, n3d, mc, md = chunks(
        core,
        b1[2:] + b3[:2] + b1[:2] + b3[2:] + b0,
        r1[2:] + r3[:2] + r1[:2] + r3[2:] + r0,
        tile,
        own_y,
        other_y,
    )
    up_d, down_c = along_y(n1d, 1), along_y(n3c, -1)
    up_a, down_b = along_x(n1a + u, 1), along_x(n3b + v, -1)
    up_c, down_d = along_y(n1c + w, 1), along_y(n3d + q, -1)
    front = second_ring(meet(y, ma, mb, up_a, up_b, down_a, down_b), along_y)
    back = second_ring(meet(x, mc, md, up_c, up_d, down_c, down_d), along_x)

    by_z = tile.reshape(8, 8, 32, 512)

    def rows_of(target):
        return lax.dynamic_index_in_dim(by_z, lax.rem(target, 8), 1, keepdims=False).reshape(256, 512)

    pair = jnp.where(z < 2, jnp.stack([rows_of(z), rows_of(z + 1)]), 0.0)
    for k in (2, 4, 6):
        pair = pair + move(
            jnp.stack([rows_of(z + k), rows_of(z + k + 1)]),
            lambda px, py, pz, k=k: (px, py, pz + k) if pz < 2 else None,
        )
    came = along_z(pair[1], 1)
    even = lax.rem(z, 2) == 0
    newest = jnp.where(even, pair[0], came)
    oldest = jnp.where(even, came, pair[0])
    other = swap_half(jnp.stack([newest, oldest]))
    w0 = jnp.where(half == 0, newest, other[0])
    w1 = jnp.where(half == 0, other[0], newest)
    w2 = jnp.where(half == 0, oldest, other[1])
    weights = [w0, w1, w2]

    spread = z_exchange(jnp.concatenate([front, back], axis=1).reshape(8, 32, 512))
    drive, rest = call(drives_kernel, [(8, 32, 128), (3, 32, 128)], spread, mine)

    adjoints, turned = [], []
    for step in range(4):
        if step:
            terms = []
            for k in range(step):
                terms += [weights[k], *turned[step - 1 - k]]
            coupled = call(coupled_kernel, (8, 32, 128), core[None], *terms)
            drive = call(
                lambda *refs, step=step: drive_kernel(*refs, step=step),
                (8, 32, 128),
                col_exchange(coupled),
                rest,
            )
        lying, plain = call(inverse_kernel, [(256, 128), (128, 256)], z_exchange(drive), self_inverse)
        adjoints.append(plain)
        if step < 3:
            turned.append((lying, swap_core(lying)))

    def whole(part):
        theirs = swap_half(part)
        return jnp.concatenate(
            [jnp.where(half == 0, part, theirs), jnp.where(half == 0, theirs, part)], axis=1
        )

    return jnp.concatenate([whole(jnp.stack(adjoints[:3])), whole(adjoints[3][None])], axis=0)


def solution(mesh):
    placed = (
        P("delay", "row", None, "col"),
        P("delay", None, ("row", "col")),
        P(None, None, ("row", "col")),
        P(("row", "col"), None, None),
    )
    return jax.shard_map(
        on_device,
        mesh=mesh,
        in_specs=placed,
        out_specs=P(None, None, ("row", "col")),
        check_vma=False,
    )
```
